32 devices in a mesh: dp: 4 (over z), mp: 8 (over y, x, core).
Axes of the slice: x: 2, y: 2, z: 4, core: 2. Of those that a mesh axis runs over, the one named last changes fastest.
Arguments:
- features: bfloat16 [192, 1664], P('dp'), may hold values from -6 to 6
- output_grad: bfloat16 [192, 1664], P('dp'), may hold values from -6 to 6
- send_rows: int32 [16, 12], P('dp'), may hold values from 0 to 48, as said below
- patches: int32 [16], replicated, may hold values from 0 to 12, as said below
- up_weight: float32 [6144, 1664], P(('dp', 'mp'))
- down_weight: float32 [6144, 1664], P(('dp', 'mp'))
- up_moment: float32 [6144, 1664], P(('dp', 'mp')), may hold values from -0.0006 to 0.0006
- down_moment: float32 [6144, 1664], P(('dp', 'mp')), may hold values from -0.0006 to 0.0006
- up_second: float32 [6144, 1664], P(('dp', 'mp')), may hold values from 1e-09 to 1e-07
- down_second: float32 [6144, 1664], P(('dp', 'mp')), may hold values from 1e-09 to 1e-07
Outputs:
- new_up: float32 [6144, 1664], P(('dp', 'mp'))
- new_down: float32 [6144, 1664], P(('dp', 'mp'))
- ratios: float32 [2], replicated
The draws below stay inside these ranges and needn't reach their ends.
Inputs may be any that keep to these rules, and one draw needn't show every extreme that they name: `send_rows`: row d * 4 + p lists the rows of group d's block sent to group p, one a slot, 48 marking an empty slot. Group d's live rows are the first ones of its block, as many as the sum of its 4 patch counts; each live row is listed exactly once in group d's rows and no other row is listed. In every draw some group fills all its slots. `patches`: entries d * 4 to d * 4 + 3 are the patch counts of group d's images, 0 for an empty place; in every draw some group's counts sum to 48.
All inputs are finite; a program needn't handle non-finite values.
Results may differ from the reference program's by a relative error of at most 0.0003.
Values may be sent and summed in bfloat16 or wider, within the bound.
No kernel may reach another device: no remote copies, remote signals or barrier semaphores. Data moves between devices by JAX's collectives and lax.ppermute only.
A program may use at most 64 MiB of HBM per device.

```python
import math
import jax
import jax.numpy as jnp
from jax import lax

D = 1664
FF = 6144
IMGS = 4
S = 12
CAP = 48
MAXP = 12
TOKENS = 192
N_DP = 4


def lists_and_counts(key):
    base = jax.random.fold_in(key, 11)
    first, second, third, fourth = jax.random.split(base, 4)
    heavy = jax.random.randint(first, (), 0, N_DP)
    groups = jnp.arange(N_DP, dtype=jnp.int32)
    active = jax.random.randint(second, (N_DP,), 1, IMGS + 1)
    active = jnp.where(groups == heavy, IMGS, active)
    counts = jax.random.randint(third, (N_DP, IMGS), max(MAXP // 4, 1), MAXP + 1)
    counts = jnp.where(jnp.arange(IMGS)[None, :] < active[:, None], counts, 0)
    counts = jnp.where((groups == heavy)[:, None], MAXP, counts).astype(jnp.int32)
    live = jnp.sum(counts, axis=1)

    def one_order(subkey):
        return jax.random.permutation(subkey, CAP)
    ranks = jax.vmap(one_order)(jax.random.split(fourth, N_DP))
    positions = jnp.arange(CAP, dtype=jnp.int32)[None, :]
    score = jnp.where(positions < live[:, None], 0, CAP) + ranks
    order = jnp.argsort(score, axis=1, stable=True).astype(jnp.int32)
    peers = jnp.arange(N_DP, dtype=jnp.int32)
    slots = jnp.arange(S, dtype=jnp.int32)
    index = slots[None, None, :] * N_DP + jnp.mod(peers[None, :, None] - groups[:, None, None], N_DP)
    picked = jnp.take_along_axis(order, index.reshape(N_DP, N_DP * S), axis=1).reshape(N_DP, N_DP, S)
    listed = jnp.where(index < live[:, None, None], picked, CAP)
    return (listed.reshape(N_DP * N_DP, S).astype(jnp.int32), counts.reshape(N_DP * IMGS))


def draw_send_rows(key, part):
    return lists_and_counts(key)[0]


def draw_patches(key, part):
    return lists_and_counts(key)[1]


def rising_rows(key, salt):
    first, second = jax.random.split(jax.random.fold_in(key, salt))
    rows = jnp.arange(FF, dtype=jnp.float32)
    base = jnp.sqrt(1.0 + 2.0 * rows / (FF - 1))
    factor = jnp.exp(jax.random.uniform(first, (FF, 1), jnp.float32, -0.35, 0.35))
    values = jax.random.normal(second, (FF, D), jnp.float32)
    return (values * factor * base[:, None]).astype(jnp.float32)


def draw_up_weight(key, part):
    return rising_rows(key, 23)


def draw_down_weight(key, part):
    return rising_rows(key, 29)


def block_scale(key, dims, cuts, low, largest):
    factor_of, own = 1.0, jax.random.fold_in(key, 6)
    for axis_at, parts in cuts:
        heights = jnp.exp(jax.random.uniform(jax.random.fold_in(own, axis_at), (parts,), jnp.float32, low / len(cuts), largest / len(cuts)))
        factor_of = factor_of * jnp.repeat(heights, dims[axis_at] // parts).reshape([-1 if axis == axis_at else 1 for axis in range(len(dims))])
    return factor_of


def noise(key, shape, deviation, reach, shards=(), kind=jnp.bfloat16):
    level = block_scale(key, shape, shards, -0.22, 0.18) if shards else 1.0
    result = jax.random.normal(key, shape, jnp.float32) * deviation * level
    return jnp.minimum(jnp.maximum(result, -reach), reach).astype(kind)


def setup_inputs(seed: int = 0) -> dict:
    arg_keys = jax.random.split(jax.random.key(seed), 11)
    return {
        "features": noise(arg_keys[0], (TOKENS, D), 1.0, 6.0, ((0, 4),)),
        "output_grad": noise(arg_keys[1], (TOKENS, D), 1.0, 6.0, ((0, 4),)),
        "send_rows": draw_send_rows(jax.random.fold_in(arg_keys[10], 71), 0),
        "patches": draw_patches(jax.random.fold_in(arg_keys[10], 71), 0),
        "up_weight": draw_up_weight(jax.random.fold_in(arg_keys[10], 71), 0),
        "down_weight": draw_down_weight(jax.random.fold_in(arg_keys[10], 71), 0),
        "up_moment": noise(arg_keys[6], (FF, D), 0.0001, 0.0006, ((0, 32),), jnp.float32),
        "down_moment": noise(arg_keys[7], (FF, D), 0.0001, 0.0006, ((0, 32),), jnp.float32),
        "up_second": jnp.clip(jnp.exp(math.log(1.0000000116860974e-07) - 4.6051702 * jax.random.uniform(arg_keys[8], (FF, D), jnp.float32) ** block_scale(arg_keys[8], (FF, D), ((0, 32),), -0.2, 0.2)), 9.999999717180685e-10, 1.0000000116860974e-07),
        "down_second": jnp.clip(jnp.exp(math.log(1.0000000116860974e-07) - 4.6051702 * jax.random.uniform(arg_keys[9], (FF, D), jnp.float32) ** block_scale(arg_keys[9], (FF, D), ((0, 32),), -0.2, 0.2)), 9.999999717180685e-10, 1.0000000116860974e-07),
    }


inv_root_two = 1.0 / math.sqrt(2.0)
inv_root_tau = 1.0 / math.sqrt(2.0 * math.pi)
beta_first = 0.9
beta_second = 0.999
corr_first = 0.99997343860111
corr_second = 0.09520785288629
adam_eps = 1e-06
norm_eps = 1e-06
decay_rate = 0.05
learn_rate = 0.02

def gelu_exact(value):
    return 0.5 * value * (1.0 + lax.erf(value * inv_root_two))

def gelu_slope(value):
    return 0.5 * (1.0 + lax.erf(value * inv_root_two)) + value * jnp.exp(-0.5 * value * value) * inv_root_tau

def lamb_update(weight, grad, moment, second):
    moment_new = beta_first * moment + (1.0 - beta_first) * grad
    second_new = beta_second * second + (1.0 - beta_second) * grad * grad
    return moment_new / corr_first / (jnp.sqrt(second_new / corr_second) + adam_eps) + decay_rate * weight

def reference(features, output_grad, send_rows, patches, up_weight, down_weight, up_moment, down_moment, up_second, down_second):
    total = jnp.sum(patches).astype(jnp.float32)
    up_scale = 1.0 / math.sqrt(D)
    down_scale = 1.0 / math.sqrt(FF)
    lists = send_rows.reshape(N_DP, N_DP, S)
    zero_rows = jnp.zeros((N_DP, 1, D), jnp.bfloat16)
    feat_pad = jnp.concatenate([features.reshape(N_DP, CAP, D), zero_rows], 1)
    grad_pad = jnp.concatenate([output_grad.reshape(N_DP, CAP, D), zero_rows], 1)
    up_half = up_weight.astype(jnp.bfloat16)
    down_half = down_weight.astype(jnp.bfloat16)
    senders = jnp.arange(N_DP, dtype=jnp.int32)[:, None]

    def group_terms(carry, target):
        index = lists[:, target, :]
        inputs = feat_pad[senders, index].reshape(N_DP * S, D)
        cotangent = grad_pad[senders, index].reshape(N_DP * S, D)
        pre = jnp.dot(inputs, up_half.T, preferred_element_type=jnp.float32) * up_scale
        hidden = gelu_exact(pre).astype(jnp.bfloat16)
        back = jnp.dot(cotangent, down_half.T, preferred_element_type=jnp.float32) * down_scale
        slope = (back * gelu_slope(pre)).astype(jnp.bfloat16)
        up_part = jnp.dot(slope.T, inputs, preferred_element_type=jnp.float32) * (up_scale / total)
        down_part = jnp.dot(hidden.T, cotangent, preferred_element_type=jnp.float32) * (down_scale / total)
        return ((carry[0] + up_part, carry[1] + down_part), None)
    zeros = jnp.zeros((FF, D), jnp.float32)
    (up_grad, down_grad), _ = lax.scan(group_terms, (zeros, zeros), jnp.arange(N_DP, dtype=jnp.int32))
    update_up = lamb_update(up_weight, up_grad, up_moment, up_second)
    update_down = lamb_update(down_weight, down_grad, down_moment, down_second)
    ratio_up = jnp.sqrt(jnp.sum(up_weight * up_weight) / (jnp.sum(update_up * update_up) + norm_eps))
    ratio_down = jnp.sqrt(jnp.sum(down_weight * down_weight) / (jnp.sum(update_down * update_down) + norm_eps))
    new_up = up_weight - learn_rate * ratio_up * update_up
    new_down = down_weight - learn_rate * ratio_down * update_down
    return (new_up, new_down, jnp.stack([ratio_up, ratio_down]))
```

```python
import functools
import math

import jax
import jax.numpy as jnp
from jax import lax
from jax.experimental import pallas as pl
from jax.experimental.pallas import tpu as pltpu
from jax.sharding import PartitionSpec as P


inv_root_two = 1.0 / math.sqrt(2.0)
inv_root_tau = 1.0 / math.sqrt(2.0 * math.pi)
beta_first = 0.9
beta_second = 0.999
corr_first = 0.99997343860111
corr_second = 0.09520785288629
adam_eps = 1e-06
norm_eps = 1e-06
decay_rate = 0.05
learn_rate = 0.02


def gelu_exact(value):
    return 0.5 * value * (1.0 + lax.erf(value * inv_root_two))


def gelu_slope(value):
    return (
        0.5 * (1.0 + lax.erf(value * inv_root_two))
        + value * jnp.exp(-0.5 * value * value) * inv_root_tau
    )


def lamb_update(weight, grad, moment, second):
    moment_new = beta_first * moment + (1.0 - beta_first) * grad
    second_new = beta_second * second + (1.0 - beta_second) * grad * grad
    return (
        moment_new / corr_first / (jnp.sqrt(second_new / corr_second) + adam_eps)
        + decay_rate * weight
    )


def gather_weights(
    hidden_units,
    images,
    features,
    output_grad,
    send_rows,
    patches,
    up_weight,
    down_weight,
    up_moment,
    down_moment,
    up_second,
    down_second,
):
    width = features.shape[1]
    total = jnp.sum(patches).astype(jnp.float32)
    up_scale = 1.0 / math.sqrt(width)
    down_scale = 1.0 / math.sqrt(hidden_units)
    group = lax.axis_index("dp")
    counts = lax.dynamic_slice_in_dim(patches, group * images, images)
    live = jnp.sum(counts)
    inside = (jnp.arange(features.shape[0], dtype=jnp.int32) < live)[:, None]
    inputs = jnp.where(inside, features, jnp.zeros_like(features))
    cotangent = jnp.where(inside, output_grad, jnp.zeros_like(output_grad))
    stacked = jnp.stack([up_weight.astype(jnp.bfloat16), down_weight.astype(jnp.bfloat16)])
    piece = lax.all_gather(stacked, "dp", axis=1, tiled=True)
    pre_part = (
        lax.dot_general(
            inputs, piece[0], (((1,), (1,)), ((), ())), preferred_element_type=jnp.float32
        )
        * up_scale
    )
    back_part = (
        lax.dot_general(
            cotangent, piece[1], (((1,), (1,)), ((), ())), preferred_element_type=jnp.float32
        )
        * down_scale
    )
    both = jnp.stack([pre_part, back_part])
    pre = both[0]
    hidden = gelu_exact(pre).astype(jnp.bfloat16)
    slope = (both[1] * gelu_slope(pre)).astype(jnp.bfloat16)
    up_term = lax.dot_general(
        slope, inputs, (((0,), (0,)), ((), ())), preferred_element_type=jnp.float32
    ) * (up_scale / total)
    down_term = lax.dot_general(
        hidden, cotangent, (((0,), (0,)), ((), ())), preferred_element_type=jnp.float32
    ) * (down_scale / total)
    summed = lax.psum_scatter(
        jnp.concatenate([up_term, down_term], 1).astype(jnp.bfloat16),
        "dp",
        scatter_dimension=0,
        tiled=True,
    ).astype(jnp.float32)
    update_up = lamb_update(up_weight, summed[:, :width], up_moment, up_second)
    update_down = lamb_update(down_weight, summed[:, width:], down_moment, down_second)
    weight_up_sq, update_up_sq, weight_down_sq, update_down_sq = lax.psum(
        (
            jnp.sum(up_weight * up_weight),
            jnp.sum(update_up * update_up),
            jnp.sum(down_weight * down_weight),
            jnp.sum(update_down * update_down),
        ),
        ("dp", "mp"),
    )
    ratio_up = jnp.sqrt(weight_up_sq / (update_up_sq + norm_eps))
    ratio_down = jnp.sqrt(weight_down_sq / (update_down_sq + norm_eps))
    new_up = up_weight - learn_rate * ratio_up * update_up
    new_down = down_weight - learn_rate * ratio_down * update_down
    return (new_up, new_down, jnp.stack([ratio_up, ratio_down]))


moment_keep = beta_first / corr_first
moment_add = (1.0 - beta_first) / corr_first
second_keep = beta_second / corr_second
second_add = (1.0 - beta_second) / corr_second


def column_chunks(width):
    edges = list(range(0, width, 256)) + [width]
    return list(zip(edges[:-1], edges[1:]))


def fold_rows(block):
    rows, columns = block.shape
    part = jnp.sum(block.reshape(rows // 8, 8, columns), axis=0)
    out = part[:, :128]
    for at in range(128, columns, 128):
        out = out + part[:, at : at + 128]
    return out


def prepare_kernel(up_ref, down_ref, up_half_ref, down_half_ref, squares_ref):
    for at, (source, half) in enumerate(((up_ref, up_half_ref), (down_ref, down_half_ref))):
        acc = jnp.zeros((8, 128), jnp.float32)
        for low, high in column_chunks(source.shape[1]):
            block = source[:, low:high]
            half[:, low:high] = block.astype(jnp.bfloat16)
            acc = acc + fold_rows(block * block)
        squares_ref[at] = acc


def update_kernel(groups, devices, hidden_units, *refs):
    patches_ref, squares_ref, features_ref, grads_ref = refs[:4]
    moved = refs[4 : 4 + 2 * (groups - 1)]
    (
        up_half_ref,
        down_half_ref,
        up_ref,
        down_ref,
        up_moment_ref,
        down_moment_ref,
        up_second_ref,
        down_second_ref,
        step_up_ref,
        step_down_ref,
        sums_ref,
        inputs_ref,
        cotangent_ref,
    ) = refs[4 + 2 * (groups - 1) :]
    cap, width = features_ref.shape
    tokens = groups * cap
    images = patches_ref.shape[0] // groups
    mine = lax.axis_index("dp")
    core = lax.rem(lax.axis_index("mp"), 2)
    up_scale = 1.0 / math.sqrt(width)
    down_scale = 1.0 / math.sqrt(hidden_units)

    inputs_ref[0:cap, :] = features_ref[...]
    cotangent_ref[0:cap, :] = grads_ref[...]
    for slot in range(1, groups):
        far, near = moved[slot - 1], moved[groups - 1 + slot - 1]
        rows = slice(slot * cap, (slot + 1) * cap)

        @pl.when(core == 0)
        def _():
            inputs_ref[rows, :] = far[...]
            cotangent_ref[rows, :] = near[...]

        @pl.when(core != 0)
        def _():
            inputs_ref[rows, :] = near[...]
            cotangent_ref[rows, :] = far[...]

    total = patches_ref[0]
    for at in range(1, groups * images):
        total = total + patches_ref[at]
    column = lax.broadcasted_iota(jnp.int32, (1, tokens), 1)
    alive = column < 0
    for slot in range(groups):
        group = lax.rem(mine - slot + groups, groups)
        live = patches_ref[group * images]
        for at in range(1, images):
            live = live + patches_ref[group * images + at]
        alive = alive | ((column >= slot * cap) & (column < slot * cap + live))

    across = (((1,), (1,)), ((), ()))
    pre = (
        lax.dot_general(
            up_half_ref[...], inputs_ref[...], across, preferred_element_type=jnp.float32
        )
        * up_scale
    )
    back = (
        lax.dot_general(
            down_half_ref[...], cotangent_ref[...], across, preferred_element_type=jnp.float32
        )
        * down_scale
    )
    half_erf = 0.5 * (1.0 + lax.erf(pre * inv_root_two))
    hidden = jnp.where(alive, pre * half_erf, 0.0).astype(jnp.bfloat16)
    tail = pre * jnp.exp(-0.5 * pre * pre) * inv_root_tau
    slope = jnp.where(alive, back * (half_erf + tail), 0.0).astype(jnp.bfloat16)

    spread = jnp.full((8, 128), total.astype(jnp.float32))
    parts = []
    for scale, left, right_ref, weight_ref, moment_ref, second_ref, step_ref in (
        (up_scale, slope, inputs_ref, up_ref, up_moment_ref, up_second_ref, step_up_ref),
        (
            down_scale,
            hidden,
            cotangent_ref,
            down_ref,
            down_moment_ref,
            down_second_ref,
            step_down_ref,
        ),
    ):
        factor = (scale / spread)[0:1, 0:1]
        acc = jnp.zeros((8, 128), jnp.float32)
        for low, high in column_chunks(width):
            grad = (
                jnp.dot(left, right_ref[:, low:high], preferred_element_type=jnp.float32)
                * factor
            )
            moment = moment_keep * moment_ref[:, low:high] + moment_add * grad
            second = second_keep * second_ref[:, low:high] + second_add * grad * grad
            step = (
                moment / (jnp.sqrt(second) + adam_eps) + decay_rate * weight_ref[:, low:high]
            )
            step_ref[:, low:high] = step
            acc = acc + fold_rows(step * step)
        parts.append(acc)
    lane = lax.broadcasted_iota(jnp.int32, (1, 128), 1)
    row = jnp.zeros((1, 128), jnp.float32)
    for at, value in enumerate((squares_ref[0], parts[0], squares_ref[1], parts[1])):
        one = jnp.sum(jnp.sum(value, axis=0, keepdims=True), axis=1, keepdims=True)
        row = jnp.where(lane == at, one, row)
    sums_ref[...] = jnp.broadcast_to(row, (devices, 128))


def finish_kernel(
    sums_ref,
    up_ref,
    down_ref,
    step_up_ref,
    step_down_ref,
    new_up_ref,
    new_down_ref,
    ratios_ref,
    held_ref,
    sem_ref,
):
    sums = jnp.sum(sums_ref[...], axis=0, keepdims=True)
    copies = []
    for at, (weight_ref, step_ref, new_ref) in enumerate(
        ((up_ref, step_up_ref, new_up_ref), (down_ref, step_down_ref, new_down_ref))
    ):
        ratio = jnp.sqrt(
            sums[:, 2 * at : 2 * at + 1] / (sums[:, 2 * at + 1 : 2 * at + 2] + norm_eps)
        )
        ratios_ref[at] = ratio[0, 0]
        rows = weight_ref.shape[0]
        cut = rows // 2
        for half, low in enumerate(range(0, rows, cut)):
            held_ref[at, low : low + cut, :] = (
                weight_ref[low : low + cut, :]
                - (learn_rate * ratio) * step_ref[low : low + cut, :]
            )
            copy = pltpu.make_async_copy(
                held_ref.at[at, low : low + cut],
                new_ref.at[low : low + cut],
                sem_ref.at[at, half],
            )
            copy.start()
            copies.append(copy)
    for copy in copies:
        copy.wait()


def gather_tokens(
    groups,
    members,
    hidden_units,
    features,
    output_grad,
    send_rows,
    patches,
    up_weight,
    down_weight,
    up_moment,
    down_moment,
    up_second,
    down_second,
):
    rows, width = up_weight.shape
    cap = features.shape[0]
    devices = groups * members
    vmem = pl.BlockSpec(memory_space=pltpu.VMEM)
    smem = pl.BlockSpec(memory_space=pltpu.SMEM)
    core = lax.axis_index("mp") % 2
    piece = jnp.where(core == 0, features, output_grad)
    far = [
        lax.ppermute(piece, "dp", [(at, (at + slot) % groups) for at in range(groups)])
        for slot in range(1, groups)
    ]
    pair = [(at, at ^ 1) for at in range(members)]
    near = [lax.ppermute(block, "mp", pair) for block in far]

    half = jax.ShapeDtypeStruct((rows, width), jnp.bfloat16)
    full = jax.ShapeDtypeStruct((rows, width), jnp.float32)
    up_half, down_half, squares = pl.pallas_call(
        prepare_kernel,
        out_shape=(half, half, jax.ShapeDtypeStruct((2, 8, 128), jnp.float32)),
        in_specs=[vmem] * 2,
        out_specs=[vmem] * 3,
        name="prepare",
    )(up_weight, down_weight)
    step_up, step_down, sums = pl.pallas_call(
        functools.partial(update_kernel, groups, devices, hidden_units),
        out_shape=(full, full, jax.ShapeDtypeStruct((devices, 128), jnp.float32)),
        in_specs=[smem] + [vmem] * (3 + 2 * (groups - 1) + 8),
        out_specs=[vmem] * 3,
        scratch_shapes=[
            pltpu.VMEM((groups * cap, width), jnp.bfloat16),
            pltpu.VMEM((groups * cap, width), jnp.bfloat16),
        ],
        name="update",
    )(
        patches,
        squares,
        features,
        output_grad,
        *far,
        *near,
        up_half,
        down_half,
        up_weight,
        down_weight,
        up_moment,
        down_moment,
        up_second,
        down_second,
    )
    sums = lax.all_to_all(sums, ("dp", "mp"), 0, 0, tiled=True)
    return pl.pallas_call(
        finish_kernel,
        out_shape=(full, full, jax.ShapeDtypeStruct((2,), jnp.float32)),
        in_specs=[vmem] * 5,
        out_specs=[
            pl.BlockSpec(memory_space=pl.ANY),
            pl.BlockSpec(memory_space=pl.ANY),
            smem,
        ],
        scratch_shapes=[
            pltpu.VMEM((2, rows, width), jnp.float32),
            pltpu.SemaphoreType.DMA((2, 2)),
        ],
        name="finish",
    )(sums, up_weight, down_weight, step_up, step_down)


def solution(mesh):
    groups, members = mesh.shape["dp"], mesh.shape["mp"]
    spread = P(("dp", "mp"), None)
    placed = (P("dp", None), P("dp", None), P("dp", None), P()) + (spread,) * 6

    def whole(features, output_grad, send_rows, patches, up_weight, *others):
        hidden_units, width = up_weight.shape
        tokens = features.shape[0]
        if members % 2 == 0 and tokens <= hidden_units // members:
            body = functools.partial(gather_tokens, groups, members, hidden_units)
        else:
            body = functools.partial(gather_weights, hidden_units, patches.shape[0] // groups)
        return jax.shard_map(
            body,
            mesh=mesh,
            in_specs=placed,
            out_specs=(spread, spread, P()),
            check_vma=False,
        )(features, output_grad, send_rows, patches, up_weight, *others)

    return whole
```

```python
import functools
import math

import jax
import jax.numpy as jnp
from jax import lax
from jax.experimental import pallas as pl
from jax.experimental.pallas import tpu as pltpu
from jax.sharding import PartitionSpec as P


inv_root_two = 1.0 / math.sqrt(2.0)
inv_root_tau = 1.0 / math.sqrt(2.0 * math.pi)
beta_first = 0.9
beta_second = 0.999
corr_first = 0.99997343860111
corr_second = 0.09520785288629
adam_eps = 1e-06
norm_eps = 1e-06
decay_rate = 0.05
learn_rate = 0.02


def gelu_exact(value):
    return 0.5 * value * (1.0 + lax.erf(value * inv_root_two))


def gelu_slope(value):
    return (
        0.5 * (1.0 + lax.erf(value * inv_root_two))
        + value * jnp.exp(-0.5 * value * value) * inv_root_tau
    )


def lamb_update(weight, grad, moment, second):
    moment_new = beta_first * moment + (1.0 - beta_first) * grad
    second_new = beta_second * second + (1.0 - beta_second) * grad * grad
    return (
        moment_new / corr_first / (jnp.sqrt(second_new / corr_second) + adam_eps)
        + decay_rate * weight
    )


def gather_weights(
    hidden_units,
    images,
    features,
    output_grad,
    send_rows,
    patches,
    up_weight,
    down_weight,
    up_moment,
    down_moment,
    up_second,
    down_second,
):
    width = features.shape[1]
    total = jnp.sum(patches).astype(jnp.float32)
    up_scale = 1.0 / math.sqrt(width)
    down_scale = 1.0 / math.sqrt(hidden_units)
    group = lax.axis_index("dp")
    counts = lax.dynamic_slice_in_dim(patches, group * images, images)
    live = jnp.sum(counts)
    inside = (jnp.arange(features.shape[0], dtype=jnp.int32) < live)[:, None]
    inputs = jnp.where(inside, features, jnp.zeros_like(features))
    cotangent = jnp.where(inside, output_grad, jnp.zeros_like(output_grad))
    stacked = jnp.stack([up_weight.astype(jnp.bfloat16), down_weight.astype(jnp.bfloat16)])
    piece = lax.all_gather(stacked, "dp", axis=1, tiled=True)
    pre_part = (
        lax.dot_general(
            inputs, piece[0], (((1,), (1,)), ((), ())), preferred_element_type=jnp.float32
        )
        * up_scale
    )
    back_part = (
        lax.dot_general(
            cotangent, piece[1], (((1,), (1,)), ((), ())), preferred_element_type=jnp.float32
        )
        * down_scale
    )
    both = jnp.stack([pre_part, back_part])
    pre = both[0]
    hidden = gelu_exact(pre).astype(jnp.bfloat16)
    slope = (both[1] * gelu_slope(pre)).astype(jnp.bfloat16)
    up_term = lax.dot_general(
        slope, inputs, (((0,), (0,)), ((), ())), preferred_element_type=jnp.float32
    ) * (up_scale / total)
    down_term = lax.dot_general(
        hidden, cotangent, (((0,), (0,)), ((), ())), preferred_element_type=jnp.float32
    ) * (down_scale / total)
    summed = lax.psum_scatter(
        jnp.concatenate([up_term, down_term], 1).astype(jnp.bfloat16),
        "dp",
        scatter_dimension=0,
        tiled=True,
    ).astype(jnp.float32)
    update_up = lamb_update(up_weight, summed[:, :width], up_moment, up_second)
    update_down = lamb_update(down_weight, summed[:, width:], down_moment, down_second)
    weight_up_sq, update_up_sq, weight_down_sq, update_down_sq = lax.psum(
        (
            jnp.sum(up_weight * up_weight),
            jnp.sum(update_up * update_up),
            jnp.sum(down_weight * down_weight),
            jnp.sum(update_down * update_down),
        ),
        ("dp", "mp"),
    )
    ratio_up = jnp.sqrt(weight_up_sq / (update_up_sq + norm_eps))
    ratio_down = jnp.sqrt(weight_down_sq / (update_down_sq + norm_eps))
    new_up = up_weight - learn_rate * ratio_up * update_up
    new_down = down_weight - learn_rate * ratio_down * update_down
    return (new_up, new_down, jnp.stack([ratio_up, ratio_down]))


moment_keep = beta_first / corr_first
moment_add = (1.0 - beta_first) / corr_first
second_keep = beta_second / corr_second
kernel_room = 16 * 2**20
second_add = (1.0 - beta_second) / corr_second


def column_chunks(width):
    edges = list(range(0, width, 256)) + [width]
    return list(zip(edges[:-1], edges[1:]))


def fold_rows(block):
    rows, columns = block.shape
    part = jnp.sum(block.reshape(rows // 8, 8, columns), axis=0)
    out = part[:, :128]
    for at in range(128, columns, 128):
        out = out + part[:, at : at + 128]
    return out


def prepare_kernel(*refs):
    sources, held = refs[:6], refs[6:12]
    halves, squares_ref, sem_ref = refs[12:14], refs[14], refs[15]
    copies = [
        pltpu.make_async_copy(source, target, sem_ref.at[at])
        for at, (source, target) in enumerate(zip(sources, held))
    ]
    for copy in copies:
        copy.start()
    for at in range(2):
        copies[at].wait()
        acc = jnp.zeros((8, 128), jnp.float32)
        for low, high in column_chunks(held[at].shape[1]):
            block = held[at][:, low:high]
            halves[at][:, low:high] = block.astype(jnp.bfloat16)
            acc = acc + fold_rows(block * block)
        squares_ref[at] = acc
    for copy in copies[2:]:
        copy.wait()


def update_kernel(groups, devices, hidden_units, *refs):
    patches_ref, squares_ref, features_ref, grads_ref = refs[:4]
    moved = refs[4 : 4 + 2 * (groups - 1)]
    (
        up_half_ref,
        down_half_ref,
        up_ref,
        down_ref,
        up_moment_ref,
        down_moment_ref,
        up_second_ref,
        down_second_ref,
        step_up_ref,
        step_down_ref,
        sums_ref,
        inputs_ref,
        cotangent_ref,
    ) = refs[4 + 2 * (groups - 1) :]
    cap, width = features_ref.shape
    tokens = groups * cap
    images = patches_ref.shape[0] // groups
    mine = lax.axis_index("dp")
    core = lax.rem(lax.axis_index("mp"), 2)
    up_scale = 1.0 / math.sqrt(width)
    down_scale = 1.0 / math.sqrt(hidden_units)

    inputs_ref[0:cap, :] = features_ref[...]
    cotangent_ref[0:cap, :] = grads_ref[...]
    for slot in range(1, groups):
        far, near = moved[slot - 1], moved[groups - 1 + slot - 1]
        rows = slice(slot * cap, (slot + 1) * cap)

        @pl.when(core == 0)
        def _():
            inputs_ref[rows, :] = far[...]
            cotangent_ref[rows, :] = near[...]

        @pl.when(core != 0)
        def _():
            inputs_ref[rows, :] = near[...]
            cotangent_ref[rows, :] = far[...]

    total = patches_ref[0]
    for at in range(1, groups * images):
        total = total + patches_ref[at]
    column = lax.broadcasted_iota(jnp.int32, (1, tokens), 1)
    alive = column < 0
    for slot in range(groups):
        group = lax.rem(mine - slot + groups, groups)
        live = patches_ref[group * images]
        for at in range(1, images):
            live = live + patches_ref[group * images + at]
        alive = alive | ((column >= slot * cap) & (column < slot * cap + live))

    across = (((1,), (1,)), ((), ()))
    pre = (
        lax.dot_general(
            up_half_ref[...], inputs_ref[...], across, preferred_element_type=jnp.float32
        )
        * up_scale
    )
    back = (
        lax.dot_general(
            down_half_ref[...], cotangent_ref[...], across, preferred_element_type=jnp.float32
        )
        * down_scale
    )
    half_erf = 0.5 * (1.0 + lax.erf(pre * inv_root_two))
    hidden = jnp.where(alive, pre * half_erf, 0.0).astype(jnp.bfloat16)
    tail = pre * jnp.exp(-0.5 * pre * pre) * inv_root_tau
    slope = jnp.where(alive, back * (half_erf + tail), 0.0).astype(jnp.bfloat16)

    spread = jnp.full((8, 128), total.astype(jnp.float32))
    parts = []
    for scale, left, right_ref, weight_ref, moment_ref, second_ref, step_ref in (
        (up_scale, slope, inputs_ref, up_ref, up_moment_ref, up_second_ref, step_up_ref),
        (
            down_scale,
            hidden,
            cotangent_ref,
            down_ref,
            down_moment_ref,
            down_second_ref,
            step_down_ref,
        ),
    ):
        factor = (scale / spread)[0:1, 0:1]
        acc = jnp.zeros((8, 128), jnp.float32)
        for low, high in column_chunks(width):
            grad = (
                jnp.dot(left, right_ref[:, low:high], preferred_element_type=jnp.float32)
                * factor
            )
            moment = moment_keep * moment_ref[:, low:high] + moment_add * grad
            second = second_keep * second_ref[:, low:high] + second_add * grad * grad
            step = (
                moment / (jnp.sqrt(second) + adam_eps) + decay_rate * weight_ref[:, low:high]
            )
            step_ref[:, low:high] = step
            acc = acc + fold_rows(step * step)
        parts.append(acc)
    lane = lax.broadcasted_iota(jnp.int32, (1, 128), 1)
    row = jnp.zeros((1, 128), jnp.float32)
    for at, value in enumerate((squares_ref[0], parts[0], squares_ref[1], parts[1])):
        one = jnp.sum(jnp.sum(value, axis=0, keepdims=True), axis=1, keepdims=True)
        row = jnp.where(lane == at, one, row)
    sums_ref[...] = jnp.broadcast_to(row, (devices, 128))


def finish_kernel(
    sums_ref,
    up_ref,
    down_ref,
    step_up_ref,
    step_down_ref,
    new_up_ref,
    new_down_ref,
    ratios_ref,
    held_ref,
    sem_ref,
):
    sums = jnp.sum(sums_ref[...], axis=0, keepdims=True)
    copies = []
    for at, (weight_ref, step_ref, new_ref) in enumerate(
        ((up_ref, step_up_ref, new_up_ref), (down_ref, step_down_ref, new_down_ref))
    ):
        ratio = jnp.sqrt(
            sums[:, 2 * at : 2 * at + 1] / (sums[:, 2 * at + 1 : 2 * at + 2] + norm_eps)
        )
        ratios_ref[at] = ratio[0, 0]
        rows = weight_ref.shape[0]
        cut = rows // 2
        for half, low in enumerate(range(0, rows, cut)):
            held_ref[at, low : low + cut, :] = (
                weight_ref[low : low + cut, :]
                - (learn_rate * ratio) * step_ref[low : low + cut, :]
            )
            copy = pltpu.make_async_copy(
                held_ref.at[at, low : low + cut],
                new_ref.at[low : low + cut],
                sem_ref.at[at, half],
            )
            copy.start()
            copies.append(copy)
    for copy in copies:
        copy.wait()


def keep_near(value):
    return pltpu.with_memory_space_constraint(value, pltpu.VMEM)


def gather_tokens(
    groups,
    members,
    hidden_units,
    features,
    output_grad,
    send_rows,
    patches,
    up_weight,
    down_weight,
    up_moment,
    down_moment,
    up_second,
    down_second,
):
    rows, width = up_weight.shape
    cap = features.shape[0]
    devices = groups * members
    vmem = pl.BlockSpec(memory_space=pltpu.VMEM)
    smem = pl.BlockSpec(memory_space=pltpu.SMEM)
    hbm = pl.BlockSpec(memory_space=pltpu.HBM)
    core = lax.axis_index("mp") % 2
    piece = jnp.where(core == 0, features, output_grad)
    far = []
    for slot in range(1, groups):
        ring = [(at, (at + slot) % groups) for at in range(groups)]
        far.append(lax.ppermute(piece, "dp", ring))
    pair = [(at, at ^ 1) for at in range(members)]
    near = [lax.ppermute(block, "mp", pair) for block in far]

    far = [keep_near(block) for block in far]
    near = [keep_near(block) for block in near]
    half = pltpu.VMEM((rows, width), jnp.bfloat16)
    held = pltpu.VMEM((rows, width), jnp.float32)
    weights = (up_weight, down_weight, up_moment, down_moment, up_second, down_second)
    prepare = pl.pallas_call(
        prepare_kernel,
        out_shape=(held,) * 6 + (half, half, pltpu.VMEM((2, 8, 128), jnp.float32)),
        in_specs=[hbm] * 6,
        out_specs=[vmem] * 9,
        scratch_shapes=[pltpu.SemaphoreType.DMA((6,))],
        compiler_params=pltpu.CompilerParams(vmem_limit_bytes=kernel_room),
        name="prepare",
    )
    *state, up_half, down_half, squares = prepare(
        *(pltpu.with_memory_space_constraint(value, pltpu.HBM) for value in weights)
    )
    step_up, step_down, sums = pl.pallas_call(
        functools.partial(update_kernel, groups, devices, hidden_units),
        out_shape=(held, held, pltpu.VMEM((devices, 128), jnp.float32)),
        in_specs=[smem] + [vmem] * (3 + 2 * (groups - 1) + 8),
        out_specs=[vmem] * 3,
        scratch_shapes=[
            pltpu.VMEM((groups * cap, width), jnp.bfloat16),
            pltpu.VMEM((groups * cap, width), jnp.bfloat16),
        ],
        compiler_params=pltpu.CompilerParams(vmem_limit_bytes=kernel_room),
        name="update",
    )(patches, squares, features, output_grad, *far, *near, up_half, down_half, *state)
    sums = keep_near(lax.all_to_all(sums, ("dp", "mp"), 0, 0, tiled=True))
    full = jax.ShapeDtypeStruct((rows, width), jnp.float32)
    return pl.pallas_call(
        finish_kernel,
        out_shape=(full, full, jax.ShapeDtypeStruct((2,), jnp.float32)),
        in_specs=[vmem] * 5,
        out_specs=[hbm, hbm, smem],
        scratch_shapes=[
            pltpu.VMEM((2, rows, width), jnp.float32),
            pltpu.SemaphoreType.DMA((2, 2)),
        ],
        compiler_params=pltpu.CompilerParams(vmem_limit_bytes=kernel_room),
        name="finish",
    )(sums, state[0], state[1], step_up, step_down)


def solution(mesh):
    groups, members = mesh.shape["dp"], mesh.shape["mp"]
    spread = P(("dp", "mp"), None)
    placed = (P("dp", None), P("dp", None), P("dp", None), P()) + (spread,) * 6

    def use_tokens(tokens, hidden_units):
        return members % 2 == 0 and tokens <= hidden_units // members

    def whole(features, output_grad, send_rows, patches, up_weight, *others):
        hidden_units, _ = up_weight.shape
        tokens = features.shape[0]
        if use_tokens(tokens, hidden_units):
            body = functools.partial(gather_tokens, groups, members, hidden_units)
        else:
            body = functools.partial(gather_weights, hidden_units, patches.shape[0] // groups)
        step = jax.shard_map(
            body,
            mesh=mesh,
            in_specs=placed,
            out_specs=(spread, spread, P()),
            check_vma=False,
        )
        return step(features, output_grad, send_rows, patches, up_weight, *others)

    return whole
```

```python
import functools
import math

import jax
import jax.numpy as jnp
from jax import lax
from jax.experimental import pallas as pl
from jax.experimental.pallas import tpu as pltpu
from jax.sharding import PartitionSpec as P


inv_root_two = 1.0 / math.sqrt(2.0)
inv_root_tau = 1.0 / math.sqrt(2.0 * math.pi)
beta_first = 0.9
beta_second = 0.999
corr_first = 0.99997343860111
corr_second = 0.09520785288629
adam_eps = 1e-06
norm_eps = 1e-06
decay_rate = 0.05
learn_rate = 0.02


def gelu_exact(value):
    return 0.5 * value * (1.0 + lax.erf(value * inv_root_two))


def gelu_slope(value):
    return (
        0.5 * (1.0 + lax.erf(value * inv_root_two))
        + value * jnp.exp(-0.5 * value * value) * inv_root_tau
    )


def lamb_update(weight, grad, moment, second):
    moment_new = beta_first * moment + (1.0 - beta_first) * grad
    second_new = beta_second * second + (1.0 - beta_second) * grad * grad
    return (
        moment_new / corr_first / (jnp.sqrt(second_new / corr_second) + adam_eps)
        + decay_rate * weight
    )


def gather_weights(
    hidden_units,
    images,
    features,
    output_grad,
    send_rows,
    patches,
    up_weight,
    down_weight,
    up_moment,
    down_moment,
    up_second,
    down_second,
):
    width = features.shape[1]
    total = jnp.sum(patches).astype(jnp.float32)
    up_scale = 1.0 / math.sqrt(width)
    down_scale = 1.0 / math.sqrt(hidden_units)
    group = lax.axis_index("dp")
    counts = lax.dynamic_slice_in_dim(patches, group * images, images)
    live = jnp.sum(counts)
    inside = (jnp.arange(features.shape[0], dtype=jnp.int32) < live)[:, None]
    inputs = jnp.where(inside, features, jnp.zeros_like(features))
    cotangent = jnp.where(inside, output_grad, jnp.zeros_like(output_grad))
    stacked = jnp.stack([up_weight.astype(jnp.bfloat16), down_weight.astype(jnp.bfloat16)])
    piece = lax.all_gather(stacked, "dp", axis=1, tiled=True)
    pre_part = (
        lax.dot_general(
            inputs, piece[0], (((1,), (1,)), ((), ())), preferred_element_type=jnp.float32
        )
        * up_scale
    )
    back_part = (
        lax.dot_general(
            cotangent, piece[1], (((1,), (1,)), ((), ())), preferred_element_type=jnp.float32
        )
        * down_scale
    )
    both = jnp.stack([pre_part, back_part])
    pre = both[0]
    hidden = gelu_exact(pre).astype(jnp.bfloat16)
    slope = (both[1] * gelu_slope(pre)).astype(jnp.bfloat16)
    up_term = lax.dot_general(
        slope, inputs, (((0,), (0,)), ((), ())), preferred_element_type=jnp.float32
    ) * (up_scale / total)
    down_term = lax.dot_general(
        hidden, cotangent, (((0,), (0,)), ((), ())), preferred_element_type=jnp.float32
    ) * (down_scale / total)
    summed = lax.psum_scatter(
        jnp.concatenate([up_term, down_term], 1).astype(jnp.bfloat16),
        "dp",
        scatter_dimension=0,
        tiled=True,
    ).astype(jnp.float32)
    update_up = lamb_update(up_weight, summed[:, :width], up_moment, up_second)
    update_down = lamb_update(down_weight, summed[:, width:], down_moment, down_second)
    weight_up_sq, update_up_sq, weight_down_sq, update_down_sq = lax.psum(
        (
            jnp.sum(up_weight * up_weight),
            jnp.sum(update_up * update_up),
            jnp.sum(down_weight * down_weight),
            jnp.sum(update_down * update_down),
        ),
        ("dp", "mp"),
    )
    ratio_up = jnp.sqrt(weight_up_sq / (update_up_sq + norm_eps))
    ratio_down = jnp.sqrt(weight_down_sq / (update_down_sq + norm_eps))
    new_up = up_weight - learn_rate * ratio_up * update_up
    new_down = down_weight - learn_rate * ratio_down * update_down
    return (new_up, new_down, jnp.stack([ratio_up, ratio_down]))


moment_keep = beta_first / corr_first
moment_add = (1.0 - beta_first) / corr_first
second_keep = beta_second / corr_second
kernel_room = 16 * 2**20
second_add = (1.0 - beta_second) / corr_second


def column_chunks(width):
    edges = list(range(0, width, 256)) + [width]
    return list(zip(edges[:-1], edges[1:]))


def fold_rows(block):
    rows, columns = block.shape
    part = jnp.sum(block.reshape(rows // 8, 8, columns), axis=0)
    out = part[:, :128]
    for at in range(128, columns, 128):
        out = out + part[:, at : at + 128]
    return out


def prepare_kernel(*refs):
    sources, held = refs[:6], refs[6:8]
    halves, scaled, squares_ref = refs[8:10], refs[10:16], refs[16]
    raw, sem_ref = refs[17:21], refs[21]
    copies = [
        pltpu.make_async_copy(source, target, sem_ref.at[at])
        for at, (source, target) in enumerate(zip(sources, (*held, *raw)))
    ]
    for copy in copies:
        copy.start()
    for at in range(2):
        copies[at].wait()
        acc = jnp.zeros((8, 128), jnp.float32)
        for low, high in column_chunks(held[at].shape[1]):
            block = held[at][:, low:high]
            halves[at][:, low:high] = block.astype(jnp.bfloat16)
            scaled[at][:, low:high] = decay_rate * block
            acc = acc + fold_rows(block * block)
        squares_ref[at] = acc
    for at in range(4):
        copies[2 + at].wait()
        keep = moment_keep if at < 2 else second_keep
        scaled[2 + at][...] = keep * raw[at][...]


def update_kernel(groups, devices, hidden_units, *refs):
    patches_ref, squares_ref, features_ref, grads_ref = refs[:4]
    pieces = piece_list(groups)
    moved = refs[4 : 4 + 2 * len(pieces)]
    (
        up_half_ref,
        down_half_ref,
        up_ref,
        down_ref,
        up_moment_ref,
        down_moment_ref,
        up_second_ref,
        down_second_ref,
        step_up_ref,
        step_down_ref,
        sums_ref,
        inputs_ref,
        cotangent_ref,
    ) = refs[4 + 2 * len(pieces) :]
    cap, width = features_ref.shape
    tokens = groups * cap
    images = patches_ref.shape[0] // groups
    mine = lax.axis_index("dp")
    core = lax.rem(lax.axis_index("mp"), 2)
    up_scale = 1.0 / math.sqrt(width)
    down_scale = 1.0 / math.sqrt(hidden_units)

    inputs_ref[0:cap, :] = features_ref[...]
    cotangent_ref[0:cap, :] = grads_ref[...]
    for at, (slot, half) in enumerate(pieces):
        far, near = moved[at], moved[len(pieces) + at]
        low = slot * cap + half * (cap // 2)
        rows = slice(low, low + far.shape[0])

        @pl.when(core == 0)
        def _():
            inputs_ref[rows, :] = far[...]
            cotangent_ref[rows, :] = near[...]

        @pl.when(core != 0)
        def _():
            inputs_ref[rows, :] = near[...]
            cotangent_ref[rows, :] = far[...]

    total = patches_ref[0]
    for at in range(1, groups * images):
        total = total + patches_ref[at]
    column = lax.broadcasted_iota(jnp.int32, (1, tokens), 1)
    alive = column < 0
    for slot in range(groups):
        group = lax.bitwise_xor(mine, slot)
        live = patches_ref[group * images]
        for at in range(1, images):
            live = live + patches_ref[group * images + at]
        place = column - slot * cap
        stride = swap_stride(groups, slot) if slot else 0
        if stride:
            shift = lax.rem(lax.div(lax.axis_index("mp"), stride), 2) * (cap // 2)
            row = place + jnp.where(place < cap // 2, shift, -shift)
        else:
            row = place
        alive = alive | ((place >= 0) & (place < cap) & (row < live))

    across = (((1,), (1,)), ((), ()))
    pre = (
        lax.dot_general(
            up_half_ref[...], inputs_ref[...], across, preferred_element_type=jnp.float32
        )
        * up_scale
    )
    back = (
        lax.dot_general(
            down_half_ref[...], cotangent_ref[...], across, preferred_element_type=jnp.float32
        )
        * down_scale
    )
    half_erf = 0.5 * (1.0 + lax.erf(pre * inv_root_two))
    hidden = jnp.where(alive, pre * half_erf, 0.0).astype(jnp.bfloat16)
    tail = pre * jnp.exp(-0.5 * pre * pre) * inv_root_tau
    slope = jnp.where(alive, back * (half_erf + tail), 0.0).astype(jnp.bfloat16)

    spread = jnp.full((8, 128), total.astype(jnp.float32))
    parts = []
    for scale, left, right_ref, weight_ref, moment_ref, second_ref, step_ref in (
        (up_scale, slope, inputs_ref, up_ref, up_moment_ref, up_second_ref, step_up_ref),
        (
            down_scale,
            hidden,
            cotangent_ref,
            down_ref,
            down_moment_ref,
            down_second_ref,
            step_down_ref,
        ),
    ):
        factor = (scale / spread)[0:1, 0:1]
        moment_factor, second_factor = moment_add * factor, math.sqrt(second_add) * factor
        acc = jnp.zeros((8, 128), jnp.float32)
        for low, high in column_chunks(width):
            grad = jnp.dot(left, right_ref[:, low:high], preferred_element_type=jnp.float32)
            moment = moment_ref[:, low:high] + grad * moment_factor
            root = grad * second_factor
            second = second_ref[:, low:high] + root * root
            step = moment / (second * lax.rsqrt(second) + adam_eps) + weight_ref[:, low:high]
            step_ref[:, low:high] = step
            acc = acc + fold_rows(step * step)
        parts.append(acc)
    lane = lax.broadcasted_iota(jnp.int32, (1, 128), 1)
    row = jnp.zeros((1, 128), jnp.float32)
    for at, value in enumerate((squares_ref[0], parts[0], squares_ref[1], parts[1])):
        one = jnp.sum(jnp.sum(value, axis=0, keepdims=True), axis=1, keepdims=True)
        row = jnp.where(lane == at, one, row)
    sums_ref[...] = jnp.broadcast_to(row, (devices, 128))


def finish_kernel(
    sums_ref,
    up_ref,
    down_ref,
    step_up_ref,
    step_down_ref,
    new_up_ref,
    new_down_ref,
    ratios_ref,
    held_ref,
    pair_ref,
    sem_ref,
    pair_sem_ref,
):
    sums = jnp.sum(sums_ref[...], axis=0, keepdims=True)
    rows = up_ref.shape[0]
    cut = rows // sem_ref.shape[1]
    copies = []
    for at, (weight_ref, step_ref, new_ref) in enumerate(
        ((up_ref, step_up_ref, new_up_ref), (down_ref, step_down_ref, new_down_ref))
    ):
        ratio = jnp.sqrt(
            sums[:, 2 * at : 2 * at + 1] / (sums[:, 2 * at + 1 : 2 * at + 2] + norm_eps)
        )
        pair_ref[at] = ratio[0, 0]
        for part in range(sem_ref.shape[1]):
            here = pl.ds(part * cut, cut)
            held_ref[at, here, :] = (
                weight_ref[here, :] - (learn_rate * ratio) * step_ref[here, :]
            )
            copy = pltpu.make_async_copy(
                held_ref.at[at, here], new_ref.at[here], sem_ref.at[at, part]
            )
            copy.start()
            copies.append(copy)
    copies.append(pltpu.make_async_copy(pair_ref, ratios_ref, pair_sem_ref))
    copies[-1].start()
    for copy in copies:
        copy.wait()


def swap_stride(groups, slot):
    return 2 if slot == groups - 1 else 0


def slot_order(groups):
    return [groups - 1, *range(1, groups - 1)]


def piece_list(groups):
    return [
        (slot, half)
        for slot in slot_order(groups)
        for half in range(2 if swap_stride(groups, slot) else 1)
    ]


def keep_near(value):
    return pltpu.with_memory_space_constraint(value, pltpu.VMEM)


def gather_tokens(
    groups,
    members,
    hidden_units,
    features,
    output_grad,
    send_rows,
    patches,
    up_weight,
    down_weight,
    up_moment,
    down_moment,
    up_second,
    down_second,
):
    rows, width = up_weight.shape
    cap = features.shape[0]
    devices = groups * members
    vmem = pl.BlockSpec(memory_space=pltpu.VMEM)
    smem = pl.BlockSpec(memory_space=pltpu.SMEM)
    hbm = pl.BlockSpec(memory_space=pltpu.HBM)
    member = lax.axis_index("mp")
    piece = jnp.where(member % 2 == 0, features, output_grad)
    pair = [(at, at ^ 1) for at in range(members)]
    far, near = [], []
    for slot in slot_order(groups):
        stride = swap_stride(groups, slot)
        sent = piece
        if stride:
            side = member // stride % 2
            sent = lax.dynamic_slice_in_dim(piece, side * (cap // 2), cap // 2)
        swap = [(at, at ^ slot) for at in range(groups)]
        blocks = [lax.ppermute(sent, "dp", swap)]
        if stride:
            across = [(at, at ^ stride) for at in range(members)]
            blocks.append(lax.ppermute(blocks[0], "mp", across))
        for half, block in enumerate(blocks):
            near.append(lax.ppermute(block, "mp", pair))
            far.append(block)
    far = [keep_near(block) for block in far]
    near = [keep_near(block) for block in near]
    half = pltpu.VMEM((rows, width), jnp.bfloat16)
    held = pltpu.VMEM((rows, width), jnp.float32)
    weights = (up_weight, down_weight, up_moment, down_moment, up_second, down_second)
    prepare = pl.pallas_call(
        prepare_kernel,
        out_shape=(held, held, half, half) + (held,) * 6 + (pltpu.VMEM((2, 8, 128), jnp.float32),),
        in_specs=[hbm] * 6,
        out_specs=[vmem] * 11,
        scratch_shapes=[held] * 4 + [pltpu.SemaphoreType.DMA((6,))],
        compiler_params=pltpu.CompilerParams(vmem_limit_bytes=kernel_room),
        name="prepare",
    )
    near_up, near_down, up_half, down_half, *scaled, squares = prepare(
        *(pltpu.with_memory_space_constraint(value, pltpu.HBM) for value in weights)
    )
    step_up, step_down, sums = pl.pallas_call(
        functools.partial(update_kernel, groups, devices, hidden_units),
        out_shape=(held, held, pltpu.VMEM((devices, 128), jnp.float32)),
        in_specs=[smem] + [vmem] * (3 + 2 * len(far) + 8),
        out_specs=[vmem] * 3,
        scratch_shapes=[
            pltpu.VMEM((groups * cap, width), jnp.bfloat16),
            pltpu.VMEM((groups * cap, width), jnp.bfloat16),
        ],
        compiler_params=pltpu.CompilerParams(vmem_limit_bytes=kernel_room),
        name="update",
    )(patches, squares, features, output_grad, *far, *near, up_half, down_half, *scaled)
    sums = keep_near(lax.all_to_all(sums, ("dp", "mp"), 0, 0, tiled=True))
    full = jax.ShapeDtypeStruct((rows, width), jnp.float32)
    return pl.pallas_call(
        finish_kernel,
        out_shape=(full, full, jax.ShapeDtypeStruct((2,), jnp.float32)),
        in_specs=[vmem] * 5,
        out_specs=[hbm] * 3,
        scratch_shapes=[
            pltpu.VMEM((2, rows, width), jnp.float32),
            pltpu.SMEM((2,), jnp.float32),
            pltpu.SemaphoreType.DMA((2, 6)),
            pltpu.SemaphoreType.DMA,
        ],
        compiler_params=pltpu.CompilerParams(vmem_limit_bytes=kernel_room),
        name="finish",
    )(sums, near_up, near_down, step_up, step_down)


def solution(mesh):
    groups, members = mesh.shape["dp"], mesh.shape["mp"]
    spread = P(("dp", "mp"), None)
    placed = (P("dp", None), P("dp", None), P("dp", None), P()) + (spread,) * 6

    def use_tokens(tokens, hidden_units):
        paired = members % 4 == 0 and groups > 2 and groups & (groups - 1) == 0
        return paired and tokens <= hidden_units // members

    def whole(features, output_grad, send_rows, patches, up_weight, *others):
        hidden_units, _ = up_weight.shape
        tokens = features.shape[0]
        if use_tokens(tokens, hidden_units):
            body = functools.partial(gather_tokens, groups, members, hidden_units)
        else:
            body = functools.partial(gather_weights, hidden_units, patches.shape[0] // groups)
        step = jax.shard_map(
            body,
            mesh=mesh,
            in_specs=placed,
            out_specs=(spread, spread, P()),
            check_vma=False,
        )
        return step(features, output_grad, send_rows, patches, up_weight, *others)

    return whole
```

```python
import functools
import math

import jax
import jax.numpy as jnp
from jax import lax
from jax.experimental import pallas as pl
from jax.experimental.pallas import tpu as pltpu
from jax.sharding import PartitionSpec as P


inv_root_two = 1.0 / math.sqrt(2.0)
inv_root_tau = 1.0 / math.sqrt(2.0 * math.pi)
beta_first = 0.9
beta_second = 0.999
corr_first = 0.99997343860111
corr_second = 0.09520785288629
adam_eps = 1e-06
norm_eps = 1e-06
decay_rate = 0.05
learn_rate = 0.02


def gelu_exact(value):
    return 0.5 * value * (1.0 + lax.erf(value * inv_root_two))


def gelu_slope(value):
    return (
        0.5 * (1.0 + lax.erf(value * inv_root_two))
        + value * jnp.exp(-0.5 * value * value) * inv_root_tau
    )


def lamb_update(weight, grad, moment, second):
    moment_new = beta_first * moment + (1.0 - beta_first) * grad
    second_new = beta_second * second + (1.0 - beta_second) * grad * grad
    return (
        moment_new / corr_first / (jnp.sqrt(second_new / corr_second) + adam_eps)
        + decay_rate * weight
    )


def gather_weights(
    hidden_units,
    images,
    features,
    output_grad,
    send_rows,
    patches,
    up_weight,
    down_weight,
    up_moment,
    down_moment,
    up_second,
    down_second,
):
    width = features.shape[1]
    total = jnp.sum(patches).astype(jnp.float32)
    up_scale = 1.0 / math.sqrt(width)
    down_scale = 1.0 / math.sqrt(hidden_units)
    group = lax.axis_index("dp")
    counts = lax.dynamic_slice_in_dim(patches, group * images, images)
    live = jnp.sum(counts)
    inside = (jnp.arange(features.shape[0], dtype=jnp.int32) < live)[:, None]
    inputs = jnp.where(inside, features, jnp.zeros_like(features))
    cotangent = jnp.where(inside, output_grad, jnp.zeros_like(output_grad))
    stacked = jnp.stack([up_weight.astype(jnp.bfloat16), down_weight.astype(jnp.bfloat16)])
    piece = lax.all_gather(stacked, "dp", axis=1, tiled=True)
    pre_part = (
        lax.dot_general(
            inputs, piece[0], (((1,), (1,)), ((), ())), preferred_element_type=jnp.float32
        )
        * up_scale
    )
    back_part = (
        lax.dot_general(
            cotangent, piece[1], (((1,), (1,)), ((), ())), preferred_element_type=jnp.float32
        )
        * down_scale
    )
    both = jnp.stack([pre_part, back_part])
    pre = both[0]
    hidden = gelu_exact(pre).astype(jnp.bfloat16)
    slope = (both[1] * gelu_slope(pre)).astype(jnp.bfloat16)
    up_term = lax.dot_general(
        slope, inputs, (((0,), (0,)), ((), ())), preferred_element_type=jnp.float32
    ) * (up_scale / total)
    down_term = lax.dot_general(
        hidden, cotangent, (((0,), (0,)), ((), ())), preferred_element_type=jnp.float32
    ) * (down_scale / total)
    summed = lax.psum_scatter(
        jnp.concatenate([up_term, down_term], 1).astype(jnp.bfloat16),
        "dp",
        scatter_dimension=0,
        tiled=True,
    ).astype(jnp.float32)
    update_up = lamb_update(up_weight, summed[:, :width], up_moment, up_second)
    update_down = lamb_update(down_weight, summed[:, width:], down_moment, down_second)
    weight_up_sq, update_up_sq, weight_down_sq, update_down_sq = lax.psum(
        (
            jnp.sum(up_weight * up_weight),
            jnp.sum(update_up * update_up),
            jnp.sum(down_weight * down_weight),
            jnp.sum(update_down * update_down),
        ),
        ("dp", "mp"),
    )
    ratio_up = jnp.sqrt(weight_up_sq / (update_up_sq + norm_eps))
    ratio_down = jnp.sqrt(weight_down_sq / (update_down_sq + norm_eps))
    new_up = up_weight - learn_rate * ratio_up * update_up
    new_down = down_weight - learn_rate * ratio_down * update_down
    return (new_up, new_down, jnp.stack([ratio_up, ratio_down]))


moment_keep = beta_first / corr_first
moment_add = (1.0 - beta_first) / corr_first
second_keep = beta_second / corr_second
kernel_room = 16 * 2**20
second_add = (1.0 - beta_second) / corr_second


def column_chunks(width):
    edges = list(range(0, width, 256)) + [width]
    return list(zip(edges[:-1], edges[1:]))


def fold_rows(block):
    rows, columns = block.shape
    part = jnp.sum(block.reshape(rows // 8, 8, columns), axis=0)
    out = part[:, :128]
    for at in range(128, columns, 128):
        out = out + part[:, at : at + 128]
    return out


def prepare_kernel(*refs):
    sources, held = refs[:6], refs[6:8]
    halves, scaled, squares_ref = refs[8:10], refs[10:16], refs[16]
    raw, sem_ref = refs[17:21], refs[21]
    copies = [
        pltpu.make_async_copy(source, target, sem_ref.at[at])
        for at, (source, target) in enumerate(zip(sources, (*held, *raw)))
    ]
    for copy in copies:
        copy.start()
    for at in range(2):
        copies[at].wait()
        acc = jnp.zeros((8, 128), jnp.float32)
        for low, high in column_chunks(held[at].shape[1]):
            block = held[at][:, low:high]
            halves[at][:, low:high] = block.astype(jnp.bfloat16)
            scaled[at][:, low:high] = decay_rate * block
            acc = acc + fold_rows(block * block)
        squares_ref[at] = acc
    for at in range(4):
        copies[2 + at].wait()
        keep = moment_keep if at < 2 else second_keep
        scaled[2 + at][...] = keep * raw[at][...]


def update_kernel(groups, devices, hidden_units, *refs):
    patches_ref, squares_ref, features_ref, grads_ref = refs[:4]
    pieces = piece_list(groups)
    moved = refs[4 : 4 + 2 * len(pieces)]
    (
        up_half_ref,
        down_half_ref,
        up_ref,
        down_ref,
        up_moment_ref,
        down_moment_ref,
        up_second_ref,
        down_second_ref,
        step_up_ref,
        step_down_ref,
        sums_ref,
        inputs_ref,
        cotangent_ref,
    ) = refs[4 + 2 * len(pieces) :]
    cap, width = features_ref.shape
    tokens = groups * cap
    images = patches_ref.shape[0] // groups
    mine = lax.axis_index("dp")
    core = lax.rem(lax.axis_index("mp"), 2)
    up_scale = 1.0 / math.sqrt(width)
    down_scale = 1.0 / math.sqrt(hidden_units)

    inputs_ref[0:cap, :] = features_ref[...]
    cotangent_ref[0:cap, :] = grads_ref[...]
    for at, (slot, half) in enumerate(pieces):
        far, near = moved[at], moved[len(pieces) + at]
        low = slot * cap + half * (cap // 2)
        rows = slice(low, low + far.shape[0])

        inputs_ref[rows, :] = jnp.where(core == 0, far[...], near[...])
        cotangent_ref[rows, :] = jnp.where(core == 0, near[...], far[...])

    total = patches_ref[0]
    for at in range(1, groups * images):
        total = total + patches_ref[at]
    column = lax.broadcasted_iota(jnp.int32, (1, tokens), 1)
    alive = column < 0
    for slot in range(groups):
        group = lax.bitwise_xor(mine, slot)
        live = patches_ref[group * images]
        for at in range(1, images):
            live = live + patches_ref[group * images + at]
        place = column - slot * cap
        stride = swap_stride(groups, slot) if slot else 0
        if stride:
            shift = lax.rem(lax.div(lax.axis_index("mp"), stride), 2) * (cap // 2)
            row = place + jnp.where(place < cap // 2, shift, -shift)
        else:
            row = place
        alive = alive | ((place >= 0) & (place < cap) & (row < live))

    across = (((1,), (1,)), ((), ()))
    pre = (
        lax.dot_general(
            up_half_ref[...], inputs_ref[...], across, preferred_element_type=jnp.float32
        )
        * up_scale
    )
    back = (
        lax.dot_general(
            down_half_ref[...], cotangent_ref[...], across, preferred_element_type=jnp.float32
        )
        * down_scale
    )
    half_erf = 0.5 * (1.0 + lax.erf(pre * inv_root_two))
    hidden = jnp.where(alive, pre * half_erf, 0.0).astype(jnp.bfloat16)
    tail = pre * jnp.exp(-0.5 * pre * pre) * inv_root_tau
    slope = jnp.where(alive, back * (half_erf + tail), 0.0).astype(jnp.bfloat16)

    spread = jnp.full((8, 128), total.astype(jnp.float32))
    parts = []
    for scale, left, right_ref, weight_ref, moment_ref, second_ref, step_ref in (
        (up_scale, slope, inputs_ref, up_ref, up_moment_ref, up_second_ref, step_up_ref),
        (
            down_scale,
            hidden,
            cotangent_ref,
            down_ref,
            down_moment_ref,
            down_second_ref,
            step_down_ref,
        ),
    ):
        factor = (scale / spread)[0:1, 0:1]
        moment_factor, second_factor = moment_add * factor, math.sqrt(second_add) * factor
        acc = jnp.zeros((8, 128), jnp.float32)
        for low, high in column_chunks(width):
            grad = jnp.dot(left, right_ref[:, low:high], preferred_element_type=jnp.float32)
            moment = moment_ref[:, low:high] + grad * moment_factor
            root = grad * second_factor
            second = second_ref[:, low:high] + root * root
            step = moment / (second * lax.rsqrt(second) + adam_eps) + weight_ref[:, low:high]
            step_ref[:, low:high] = step
            acc = acc + fold_rows(step * step)
        parts.append(acc)
    lane = lax.broadcasted_iota(jnp.int32, (1, 128), 1)
    row = jnp.zeros((1, 128), jnp.float32)
    for at, value in enumerate((squares_ref[0], parts[0], squares_ref[1], parts[1])):
        one = jnp.sum(jnp.sum(value, axis=0, keepdims=True), axis=1, keepdims=True)
        row = jnp.where(lane == at, one, row)
    sums_ref[...] = jnp.broadcast_to(row, (devices, 128))


def finish_kernel(
    sums_ref,
    up_ref,
    down_ref,
    step_up_ref,
    step_down_ref,
    new_up_ref,
    new_down_ref,
    ratios_ref,
    held_ref,
    pair_ref,
    sem_ref,
    pair_sem_ref,
):
    sums = jnp.sum(sums_ref[...], axis=0, keepdims=True)
    rows = up_ref.shape[0]
    cut = rows // sem_ref.shape[1]
    copies = []
    for at, (weight_ref, step_ref, new_ref) in enumerate(
        ((up_ref, step_up_ref, new_up_ref), (down_ref, step_down_ref, new_down_ref))
    ):
        ratio = jnp.sqrt(
            sums[:, 2 * at : 2 * at + 1] / (sums[:, 2 * at + 1 : 2 * at + 2] + norm_eps)
        )
        pair_ref[at] = ratio[0, 0]
        for part in range(sem_ref.shape[1]):
            here = pl.ds(part * cut, cut)
            held_ref[at, here, :] = (
                weight_ref[here, :] - (learn_rate * ratio) * step_ref[here, :]
            )
            copy = pltpu.make_async_copy(
                held_ref.at[at, here], new_ref.at[here], sem_ref.at[at, part]
            )
            copy.start(priority=part % 2)
            copies.append(copy)
    copies.append(pltpu.make_async_copy(pair_ref, ratios_ref, pair_sem_ref))
    copies[-1].start()
    for copy in copies:
        copy.wait()


def swap_stride(groups, slot):
    return 2 if slot == groups - 1 else 0


def slot_order(groups):
    return [groups - 1, *range(1, groups - 1)]


def piece_list(groups):
    return [
        (slot, half)
        for slot in slot_order(groups)
        for half in range(2 if swap_stride(groups, slot) else 1)
    ]


def keep_near(value):
    return pltpu.with_memory_space_constraint(value, pltpu.VMEM)


def gather_tokens(
    groups,
    members,
    hidden_units,
    features,
    output_grad,
    send_rows,
    patches,
    up_weight,
    down_weight,
    up_moment,
    down_moment,
    up_second,
    down_second,
):
    rows, width = up_weight.shape
    cap = features.shape[0]
    devices = groups * members
    vmem = pl.BlockSpec(memory_space=pltpu.VMEM)
    smem = pl.BlockSpec(memory_space=pltpu.SMEM)
    hbm = pl.BlockSpec(memory_space=pltpu.HBM)
    member = lax.axis_index("mp")
    piece = jnp.where(member % 2 == 0, features, output_grad)
    pair = [(at, at ^ 1) for at in range(members)]
    far, near = [], []
    for slot in slot_order(groups):
        stride = swap_stride(groups, slot)
        sent = piece
        if stride:
            side = member // stride % 2
            sent = lax.dynamic_slice_in_dim(piece, side * (cap // 2), cap // 2)
        swap = [(at, at ^ slot) for at in range(groups)]
        blocks = [lax.ppermute(sent, "dp", swap)]
        if stride:
            across = [(at, at ^ stride) for at in range(members)]
            blocks.append(lax.ppermute(blocks[0], "mp", across))
        for half, block in enumerate(blocks):
            near.append(lax.ppermute(block, "mp", pair))
            far.append(block)
    far = [keep_near(block) for block in far]
    near = [keep_near(block) for block in near]
    half = pltpu.VMEM((rows, width), jnp.bfloat16)
    held = pltpu.VMEM((rows, width), jnp.float32)
    weights = (up_weight, down_weight, up_moment, down_moment, up_second, down_second)
    prepare = pl.pallas_call(
        prepare_kernel,
        out_shape=(held, held, half, half) + (held,) * 6 + (pltpu.VMEM((2, 8, 128), jnp.float32),),
        in_specs=[hbm] * 6,
        out_specs=[vmem] * 11,
        scratch_shapes=[held] * 4 + [pltpu.SemaphoreType.DMA((6,))],
        compiler_params=pltpu.CompilerParams(vmem_limit_bytes=kernel_room),
        name="prepare",
    )
    near_up, near_down, up_half, down_half, *scaled, squares = prepare(
        *(pltpu.with_memory_space_constraint(value, pltpu.HBM) for value in weights)
    )
    step_up, step_down, sums = pl.pallas_call(
        functools.partial(update_kernel, groups, devices, hidden_units),
        out_shape=(held, held, pltpu.VMEM((devices, 128), jnp.float32)),
        in_specs=[smem] + [vmem] * (3 + 2 * len(far) + 8),
        out_specs=[vmem] * 3,
        scratch_shapes=[
            pltpu.VMEM((groups * cap, width), jnp.bfloat16),
            pltpu.VMEM((groups * cap, width), jnp.bfloat16),
        ],
        compiler_params=pltpu.CompilerParams(vmem_limit_bytes=kernel_room),
        name="update",
    )(patches, squares, features, output_grad, *far, *near, up_half, down_half, *scaled)
    sums = keep_near(lax.all_to_all(sums, ("dp", "mp"), 0, 0, tiled=True))
    full = jax.ShapeDtypeStruct((rows, width), jnp.float32)
    return pl.pallas_call(
        finish_kernel,
        out_shape=(full, full, jax.ShapeDtypeStruct((2,), jnp.float32)),
        in_specs=[vmem] * 5,
        out_specs=[hbm] * 3,
        scratch_shapes=[
            pltpu.VMEM((2, rows, width), jnp.float32),
            pltpu.SMEM((2,), jnp.float32),
            pltpu.SemaphoreType.DMA((2, 3)),
            pltpu.SemaphoreType.DMA,
        ],
        compiler_params=pltpu.CompilerParams(vmem_limit_bytes=kernel_room),
        name="finish",
    )(sums, near_up, near_down, step_up, step_down)


def solution(mesh):
    groups, members = mesh.shape["dp"], mesh.shape["mp"]
    spread = P(("dp", "mp"), None)
    placed = (P("dp", None), P("dp", None), P("dp", None), P()) + (spread,) * 6

    def use_tokens(tokens, hidden_units):
        paired = members % 4 == 0 and groups > 2 and groups & (groups - 1) == 0
        return paired and tokens <= hidden_units // members

    def whole(features, output_grad, send_rows, patches, up_weight, *others):
        hidden_units, _ = up_weight.shape
        tokens = features.shape[0]
        if use_tokens(tokens, hidden_units):
            body = functools.partial(gather_tokens, groups, members, hidden_units)
        else:
            body = functools.partial(gather_weights, hidden_units, patches.shape[0] // groups)
        step = jax.shard_map(
            body,
            mesh=mesh,
            in_specs=placed,
            out_specs=(spread, spread, P()),
            check_vma=False,
        )
        return step(features, output_grad, send_rows, patches, up_weight, *others)

    return whole
```
